32 devices in a mesh: grp: 2 (over y), pre: 4 (over z), stg: 2 (over x), tp: 2 (over core).
Axes of the slice: x: 2, y: 2, z: 4, core: 2. Of those that a mesh axis runs over, the one named last changes fastest.
Arguments:
- queries: bfloat16 [32, 256, 4096], P(('grp', 'pre'), 'stg', 'tp'), parts along dimension 0, may hold values from -6 to 6
- doc_keys: bfloat16 [32, 256, 512], P(('grp', 'pre'), 'stg', 'tp'), parts along dimension 0, may hold values from -6 to 6
- doc_values: bfloat16 [32, 256, 512], P(('grp', 'pre'), 'stg', 'tp'), parts along dimension 0, may hold values from -48 to 48
- prefix_keys: bfloat16 [8, 1024, 512], P(('grp', 'pre'), None, 'tp'), parts along dimension 0, may hold values from -6 to 6
- prefix_values: bfloat16 [8, 1024, 512], P(('grp', 'pre'), None, 'tp'), parts along dimension 0, may hold values from -48 to 48
- template: int32 [32, 1], P(('grp', 'pre')), parts along dimension 0, may hold values from 0 to 3; in each aligned block of 4 rows (0 to 3, 4 to 7, ...) no two rows name the same one
- owner_table: int32 [8], P('grp'), parts along dimension 0, may hold values from 0 to 3, each once
Outputs:
- attended: bfloat16 [32, 256, 4096], P(('grp', 'pre'), 'stg', 'tp'), parts along dimension 0
The draws below stay inside these ranges and needn't reach their ends.
There are 2 independent parts, one for each index of `grp`. The reference program is written for one: setup_inputs(seed, part) draws one part's arguments, and reference() takes and returns one part's arrays. A program takes and returns all parts, laid end to end along the dimension named above; each array names one. Nothing has to cross between parts.
Inputs may be any that keep to these rules, and one draw needn't show every extreme that they name: No template is named by more than one of the 4 documents of one index of pre. `owner_table`: each owner holds the cache of exactly one template.
All inputs are finite; a program needn't handle non-finite values.
Results may differ from the reference program's by a relative error of at most 0.0034.
Values may be sent and summed in bfloat16 or wider, within the bound.
No kernel may reach another device: no remote copies, remote signals or barrier semaphores. Data moves between devices by JAX's collectives and lax.ppermute only.
A program may use at most 128 MiB of HBM per device.

```python
import math
import jax
import jax.numpy as jnp
import numpy as np
from jax import lax

H = 32
KVH = 4
HD = 128
PREF = 1024
DOC_DEV = 4
DOCS = 16
SEQ = 256
NTEMP = 4


def draw_queries(key, part):
    drawn = jnp.clip(jax.random.normal(jax.random.fold_in(key, 11), (DOCS, SEQ, H, HD), jnp.float32), -5.5, 5.5)
    return drawn.reshape(DOCS, SEQ, H * HD).astype(jnp.bfloat16)


def draw_prefix_keys(key, part):
    drawn = jnp.clip(jax.random.normal(jax.random.fold_in(key, 21), (NTEMP, PREF, KVH, HD), jnp.float32), -5.5, 5.5)
    return drawn.reshape(NTEMP, PREF, KVH * HD).astype(jnp.bfloat16)


def draw_doc_keys(key, part):
    drawn = jnp.clip(2.5 * jax.random.normal(jax.random.fold_in(key, 31), (DOCS, SEQ, KVH, HD), jnp.float32), -6.0, 6.0)
    return drawn.reshape(DOCS, SEQ, KVH * HD).astype(jnp.bfloat16)


def steps_of(stream_key, extent, cuts, smallest, largest):
    gain = 1.0
    for dim, shards_of in cuts:
        steps = jax.random.uniform(jax.random.fold_in(jax.random.fold_in(stream_key, 6), dim), (shards_of,), jnp.float32, smallest / len(cuts), largest / len(cuts))
        gain = gain * jnp.repeat(jnp.exp(steps), extent[dim] // shards_of).reshape((-1,) + (1,) * (len(extent) - 1 - dim))
    return gain


def assign_block(stream_key, own, number, rows, count, top, limit, skew):
    sequence = jax.random.permutation(stream_key, count)
    crowded, ordinary = load_shares(count, rows * top, limit, skew, True), load_shares(count, rows * top, limit, skew, False)
    places = jnp.arange(count)

    def named(tallies, rotation):
        used = int((tallies > 0).sum())
        fixed = max(1, used // 4)
        moved = fixed + (places - fixed + rotation * (used - fixed)) % max(1, count - fixed)
        return jnp.zeros((count,), jnp.int32).at[sequence[jnp.where(places < fixed, places, moved)]].set(jnp.asarray(tallies, jnp.int32))

    tallies = jnp.where(number % 4 == 0, named(crowded, number // 4), named(ordinary, number - number // 4 - 1))
    mixed = jax.random.permutation(jax.random.fold_in(own, 3), count)
    giver, taker = mixed[0:count // 2 * 2:2], mixed[1:count // 2 * 2:2]
    slack = jnp.minimum(tallies[giver] - 1, limit - tallies[taker]) // 2
    slack = jnp.where((giver == sequence[0]) | (taker == sequence[0]) | (tallies[taker] == 0), 0, jnp.maximum(slack, 0))
    moved = jax.random.randint(jax.random.fold_in(own, 4), (count // 2,), 0, 1 << 20) % (slack + 1)
    tallies = tallies.at[giver].add(-moved).at[taker].add(moved)
    members = jnp.searchsorted(jnp.cumsum(tallies), jnp.arange(rows * top), side="right").astype(jnp.int32)
    listing = members.reshape(top, rows).T
    listing = listing[jax.random.permutation(jax.random.fold_in(own, 1), rows)]
    rotation = jax.random.randint(jax.random.fold_in(own, 2), (rows, 1), 0, top)
    return jnp.take_along_axis(listing, (jnp.arange(top)[None, :] + rotation) % top, axis=1)


def load_shares(amount, total, limit, slope, full):
    portions = [(1 << 20) // math.isqrt(standing ** slope) + 1 for standing in range(1, amount + 1)]
    largest = limit if full else min(limit, max(-(-total // amount), total * portions[0] // sum(portions)))
    least = 1 if total - largest >= amount - 1 else 0
    holding, rest = [largest] + [least] * (amount - 1), total - largest - least * (amount - 1)
    while rest > 0:
        movable = [i for i in range(1, amount) if holding[i] < largest] or [i for i in range(1, amount) if holding[i] < limit]
        mass, remaining = sum([portions[i] for i in movable]), rest
        for i in movable:
            addition = min(limit - holding[i], max(1, remaining * portions[i] // mass), rest)
            holding[i] = holding[i] + addition
            rest = rest - addition
    return np.array(holding)


def gaussian(key, shape, spread, bound, shards=(), held_as=jnp.bfloat16):
    values = spread * jax.random.normal(key, shape, jnp.float32)
    if shards:
        values = values * steps_of(key, shape, shards, -0.22, 0.18)
    return jnp.clip(values, -bound, bound).astype(held_as)


def setup_inputs(seed: int = 0, part: int = 0) -> dict:
    splits = jax.random.split(jax.random.key(seed), 8)
    part_splits = jax.random.split(jax.random.fold_in(splits[7], part), 8)
    queries = draw_queries(jax.random.fold_in(jax.random.fold_in(splits[7], part), 71), part)
    doc_keys = draw_doc_keys(jax.random.fold_in(jax.random.fold_in(splits[7], part), 71), part)
    doc_values = gaussian(part_splits[2], (DOCS, SEQ, KVH * HD), 8.0, 48.0, ((0, 4), (1, 2), (2, 2)))
    prefix_keys = draw_prefix_keys(jax.random.fold_in(jax.random.fold_in(splits[7], part), 71), part)
    prefix_values = gaussian(part_splits[4], (NTEMP, PREF, KVH * HD), 8.0, 48.0, ((0, 4), (2, 2)))
    template_keys = jax.random.split(jax.random.fold_in(part_splits[5], 1), DOCS // DOC_DEV)
    template_turns = jax.random.permutation(jax.random.fold_in(part_splits[5], 3), DOCS // DOC_DEV)
    template = jax.vmap(lambda own, number: assign_block(jax.random.fold_in(part_splits[5], 2), own, number, DOC_DEV, NTEMP, 1, 1, 2))(template_keys, template_turns).reshape((DOCS, 1))
    owner_table = jax.random.permutation(part_splits[6], NTEMP).astype(jnp.int32)
    return {"queries": queries, "doc_keys": doc_keys, "doc_values": doc_values, "prefix_keys": prefix_keys, "prefix_values": prefix_values, "template": template, "owner_table": owner_table}


def attend(queries, keys_in, values_in, visible):
    row_count = queries.shape[0]
    length = keys_in.shape[0]
    groups = H // KVH
    query_heads = queries.astype(jnp.float32).reshape(row_count, KVH, groups, HD)
    key_heads = keys_in.astype(jnp.float32).reshape(length, KVH, HD)
    value_heads = values_in.astype(jnp.float32).reshape(length, KVH, HD)
    scores = jnp.einsum("tkgh,skh->kgts", query_heads, key_heads) * (HD ** -0.5)
    scores = jnp.where(visible, scores, -1e30)
    highest = jnp.max(scores, axis=-1, keepdims=True)
    weights = jnp.where(visible, jnp.exp(scores - highest), 0.0)
    totals = jnp.sum(weights, axis=-1)
    rounded = lax.optimization_barrier(weights.astype(jnp.bfloat16)).astype(jnp.float32)
    summed = jnp.einsum("kgts,skh->tkgh", rounded, value_heads)
    output = summed / jnp.transpose(totals, (2, 0, 1))[..., None]
    log_total = jnp.transpose(highest[..., 0] + jnp.log(totals), (2, 0, 1))
    return output, log_total


def reference(queries, doc_keys, doc_values, prefix_keys, prefix_values, template, owner_table):
    holders = owner_table[template[:, 0]].astype(jnp.int32)
    positions = jnp.arange(SEQ, dtype=jnp.int32)
    causal = positions[:, None] >= positions[None, :]
    everything = jnp.ones((SEQ, PREF), dtype=jnp.bool_)

    def score_one(packed):
        doc_query, doc_key, doc_value, holder = packed
        cache_keys = lax.dynamic_index_in_dim(prefix_keys, holder, 0, keepdims=False)
        cache_values = lax.dynamic_index_in_dim(prefix_values, holder, 0, keepdims=False)
        prefix_out, prefix_log = attend(doc_query, cache_keys, cache_values, everything)
        prefix_out = lax.optimization_barrier(prefix_out.astype(jnp.bfloat16)).astype(jnp.float32)
        local_out, local_log = attend(doc_query, doc_key, doc_value, causal)
        joint_log = jnp.logaddexp(prefix_log, local_log)
        mixture = jnp.exp(prefix_log - joint_log)[..., None] * prefix_out + jnp.exp(local_log - joint_log)[..., None] * local_out
        return mixture.reshape(SEQ, H * HD).astype(jnp.bfloat16)

    return lax.map(score_one, (queries, doc_keys, doc_values, holders))
```

```python
import functools
import math

import jax
import jax.numpy as jnp
from jax import lax
from jax.experimental import pallas as pl
from jax.experimental.pallas import tpu as pltpu
from jax.sharding import PartitionSpec as P

H = 32
KVH = 4
HD = 128
GROUPS = H // KVH
STACK = 2
LOG2_SCALE = HD**-0.5 * math.log2(math.e)
HIDDEN = -1e30
ROWS_BY_FEATURES = (((1,), (1,)), ((), ()))
ROWS_BY_KEYS = (((1,), (0,)), ((), ()))


def prefix_part(rows_in, cache_keys, cache_values, kv_local):
    row_count = rows_in.shape[0]
    groups = H // KVH
    length = cache_keys.shape[0]
    query_heads = rows_in.reshape(row_count, kv_local, groups, HD)
    key_heads = cache_keys.reshape(length, kv_local, HD)
    value_heads = cache_values.reshape(length, kv_local, HD)
    scores = jnp.einsum(
        "tkgh,skh->kgts", query_heads, key_heads, preferred_element_type=jnp.float32
    ) * HD ** (-0.5)
    highest = jnp.max(scores, axis=-1, keepdims=True)
    weights = jnp.exp(scores - highest)
    totals = jnp.sum(weights, axis=-1)
    summed = jnp.einsum(
        "kgts,skh->tkgh",
        weights.astype(jnp.bfloat16),
        value_heads,
        preferred_element_type=jnp.float32,
    )
    output = summed / jnp.transpose(totals, (2, 0, 1))[..., None]
    log_total = jnp.transpose(highest[..., 0] + jnp.log(totals), (2, 0, 1))
    return (
        output.reshape(row_count, kv_local * groups * HD).astype(jnp.bfloat16),
        log_total.reshape(row_count, kv_local * groups),
    )


def gathered(queries, doc_keys, doc_values, prefix_keys, prefix_values, holders):
    kv_local = KVH // lax.axis_size("tp")
    groups = H // KVH
    docs_here, span_len, features = queries.shape
    whole_keys, whole_values = (
        lax.all_gather(prefix_keys, "pre", axis=0, tiled=True),
        lax.all_gather(prefix_values, "pre", axis=0, tiled=True),
    )

    def per_document(packed):
        doc_rows, holder = packed
        cache_keys = lax.dynamic_index_in_dim(whole_keys, holder, 0, keepdims=False)
        cache_values = lax.dynamic_index_in_dim(whole_values, holder, 0, keepdims=False)
        return prefix_part(doc_rows, cache_keys, cache_values, kv_local)

    prefix_rounded, prefix_log = lax.map(per_document, (queries, holders))
    prefix_out = prefix_rounded.astype(jnp.float32)
    query_heads = queries.reshape(docs_here, span_len, kv_local, groups, HD)
    query_pos = lax.axis_index("stg") * span_len + jnp.arange(span_len, dtype=jnp.int32)
    running_max = jnp.full((docs_here, kv_local, groups, span_len), -1e30, jnp.float32)
    key_piece = lax.all_gather(doc_keys, "stg", axis=1, tiled=True)
    value_piece = lax.all_gather(doc_values, "stg", axis=1, tiled=True)
    piece_len = key_piece.shape[1]
    key_heads = key_piece.reshape(docs_here, piece_len, kv_local, HD)
    value_heads = value_piece.reshape(docs_here, piece_len, kv_local, HD)
    scores = jnp.einsum(
        "dtkgh,dskh->dkgts", query_heads, key_heads, preferred_element_type=jnp.float32
    ) * HD ** (-0.5)
    key_pos = jnp.arange(piece_len, dtype=jnp.int32)
    visible = query_pos[:, None] >= key_pos[None, :]
    scores = jnp.where(visible, scores, -1e30)
    new_max = jnp.maximum(running_max, jnp.max(scores, axis=-1))
    weights = jnp.where(visible, jnp.exp(scores - new_max[..., None]), 0.0)
    new_sum = jnp.sum(weights, axis=-1)
    added = jnp.einsum(
        "dkgts,dskh->dkgth",
        weights.astype(jnp.bfloat16),
        value_heads,
        preferred_element_type=jnp.float32,
    )
    local_heads = jnp.transpose(added / new_sum[..., None], (0, 3, 1, 2, 4))
    local_log = jnp.transpose(new_max + jnp.log(new_sum), (0, 3, 1, 2))
    prefix_heads = prefix_out.reshape(docs_here, span_len, kv_local, groups, HD)
    prefix_log = prefix_log.reshape(docs_here, span_len, kv_local, groups)
    joint_log = jnp.logaddexp(prefix_log, local_log)
    mixture = (
        jnp.exp(prefix_log - joint_log)[..., None] * prefix_heads
        + jnp.exp(local_log - joint_log)[..., None] * local_heads
    )
    return mixture.reshape(docs_here, span_len, features).astype(jnp.bfloat16)


def attend(query, pieces, out):
    for first in range(0, GROUPS, STACK):
        heads = [slice((first + i) * HD, (first + i + 1) * HD) for i in range(STACK)]
        rows = jnp.concatenate([query[:, head] for head in heads], axis=0)
        scores, folded = [], None
        for keys, _, visible in pieces:
            score = lax.dot_general(rows, keys(), ROWS_BY_FEATURES, preferred_element_type=jnp.float32)
            if visible is not None:
                score = jnp.where(jnp.concatenate([visible] * STACK, axis=0), score, HIDDEN)
            scores.append(score)
            for at in range(0, score.shape[1], HD):
                tile = score[:, at : at + HD]
                folded = tile if folded is None else jnp.maximum(folded, tile)
        peak = jnp.max(folded, axis=-1, keepdims=True) * LOG2_SCALE
        folded, total = None, None
        for (_, values, _), score in zip(pieces, scores):
            weights = jnp.exp2(score * LOG2_SCALE - peak)
            for at in range(0, score.shape[1], HD):
                tile = weights[:, at : at + HD]
                folded = tile if folded is None else folded + tile
            added = lax.dot_general(
                weights.astype(jnp.bfloat16), values(), ROWS_BY_KEYS, preferred_element_type=jnp.float32
            )
            total = added if total is None else total + added
        result = (total / jnp.sum(folded, axis=-1, keepdims=True)).astype(jnp.bfloat16)
        span = query.shape[0]
        for i, head in enumerate(heads):
            out[:, head] = result[i * span : (i + 1) * span]


def masks(span, use_other):
    row = lax.broadcasted_iota(jnp.int32, (span, span), 0)
    column = lax.broadcasted_iota(jnp.int32, (span, span), 1)
    return row >= column, row * 0 + use_other > 0


def whole(ref):
    return lambda: ref[...]


def own_kernel(where, query, cache_keys, cache_values, keys, values, theirs, out):
    span = keys.shape[1]
    half = cache_keys.shape[1] // 2
    causal, earlier = masks(span, where[0])
    pieces = [
        (whole(cache_keys.at[0, i * half : (i + 1) * half]), whole(cache_values.at[0, i * half : (i + 1) * half]), None)
        for i in range(2)
    ]
    pieces.append((whole(keys.at[0]), whole(values.at[0]), causal))
    pieces.append((whole(theirs.at[0, 0]), whole(theirs.at[0, 1]), earlier))
    attend(query.at[0], pieces, out.at[0])


def cache_pieces(caches, merged):
    pieces = []
    for piece in caches:
        if merged:
            one, other = piece
            pieces.append(
                (
                    lambda one=one, other=other: one[0] + other[0],
                    lambda one=one, other=other: one[1] + other[1],
                    None,
                )
            )
        else:
            pieces.append((whole(piece.at[0]), whole(piece.at[1]), None))
    return pieces


def theirs_part(where, query, keys, values, theirs, pieces, out):
    causal, earlier = masks(keys.shape[1], 1 - where[0])
    pieces = pieces + [
        (whole(theirs.at[0, 0]), whole(theirs.at[0, 1]), causal),
        (whole(keys.at[0]), whole(values.at[0]), earlier),
    ]
    attend(query, pieces, out)


def mine_part(where, query, keys, values, theirs, pieces, out):
    causal, earlier = masks(keys.shape[1], where[0])
    pieces = pieces + [
        (whole(keys.at[0]), whole(values.at[0]), causal),
        (whole(theirs.at[0, 0]), whole(theirs.at[0, 1]), earlier),
    ]
    attend(query, pieces, out)


def both_kernel(counts, where, query, sent_query, keys, values, theirs, *rest):
    pieces, rest = cache_pieces(rest[:counts], False), rest[counts:]
    _, out, sent_out = rest

    @pl.when(pl.program_id(0) == 0)
    def _():
        theirs_part(where, sent_query.at[0], keys, values, theirs, pieces, sent_out)

    @pl.when(pl.program_id(0) == 1)
    def _():
        mine_part(where, query.at[0], keys, values, theirs, pieces, out.at[0])


def theirs_kernel(where, sent_query, keys, values, theirs, *rest):
    caches, (sent_out,) = rest[:-1], rest[-1:]
    pieces = cache_pieces(list(zip(caches[0::2], caches[1::2])), True)
    theirs_part(where, sent_query.at[0], keys, values, theirs, pieces, sent_out)


def mine_kernel(where, query, keys, values, theirs, *rest):
    caches, (_, out) = rest[:-2], rest[-2:]
    pieces = cache_pieces(list(zip(caches[0::2], caches[1::2])), True)
    mine_part(where, query.at[0], keys, values, theirs, pieces, out.at[0])


def cost(rows, keys, moved):
    return pl.CostEstimate(flops=4 * rows * keys * HD, transcendentals=rows * keys, bytes_accessed=moved)


def exchanged(queries, doc_keys, doc_values, prefix_keys, prefix_values, holders):
    me, stage = lax.axis_index("pre"), lax.axis_index("stg")
    owners = lax.axis_size("pre")
    docs, span, features = queries.shape
    length = prefix_keys.shape[1]
    half = length // 2
    width = GROUPS * HD
    other = 1 - stage

    def over(axis, pairs):
        return lambda block: lax.ppermute(block, axis, pairs)

    near = over("pre", [(i, i ^ 1) for i in range(owners)])
    far = over("pre", [(i, i ^ 2) for i in range(owners)])
    middle = over("pre", [(1, 2), (2, 1)])
    forward = over("pre", [(2, 3), (1, 0)])
    partner = over("stg", [(0, 1), (1, 0)])

    distance = holders ^ me
    order = jnp.arange(docs, dtype=jnp.int32)
    doc_at = [jnp.sum(jnp.where(distance == j, order, 0)) for j in range(owners)]
    where = jnp.stack([stage] + doc_at).astype(jnp.int32)

    cache = jnp.stack([prefix_keys[0], prefix_values[0]])
    cache = lax.dynamic_slice_in_dim(cache, stage * HD, HD, 2)
    first, second = cache[:, :half], cache[:, half:]
    far_first, far_second = far(first), far(second)
    near_first, near_second = near(first), near(second)

    local = jnp.stack([doc_keys, doc_values], axis=1)
    sent_local = jnp.concatenate(
        [
            lax.dynamic_slice_in_dim(local, other * HD, HD, 3),
            lax.dynamic_slice(local, (doc_at[0], 0, 0, stage * HD), (1, 2, span, HD)),
        ]
    )
    their_local = partner(sent_local)
    sent_queries = jnp.concatenate(
        [lax.dynamic_slice(queries, (doc_at[j], 0, other * width), (1, span, width)) for j in range(1, owners)]
    )
    their_queries = partner(sent_queries)

    first, far_first = lax.optimization_barrier((first, far_first))
    middle_first, forward_first = middle(first), forward(far_first)
    second, far_second = lax.optimization_barrier((second, far_second))
    middle_second, forward_second = middle(second), forward(far_second)

    def call(kernel, in_specs, out_specs, out_shape, grid, name, work, aliases=None):
        return pl.pallas_call(
            kernel,
            grid_spec=pltpu.PrefetchScalarGridSpec(
                num_scalar_prefetch=1, grid=grid, in_specs=in_specs, out_specs=out_specs
            ),
            out_shape=out_shape,
            input_output_aliases=aliases or {},
            cost_estimate=work,
            name=name,
        )

    def head(i, w):
        return jnp.where(i == 0, w[0], 1 - w[0])

    keys_all = length + 2 * span
    step_bytes = 2 * 2 * (keys_all * HD + span * width)
    answer = jax.ShapeDtypeStruct(queries.shape, jnp.bfloat16)
    out = call(
        own_kernel,
        [
            pl.BlockSpec((1, span, width), lambda i, w: (w[1], 0, head(i, w))),
            pl.BlockSpec((1, length, HD), lambda i, w: (0, 0, head(i, w))),
            pl.BlockSpec((1, length, HD), lambda i, w: (0, 0, head(i, w))),
            pl.BlockSpec((1, span, HD), lambda i, w: (w[1], 0, head(i, w))),
            pl.BlockSpec((1, span, HD), lambda i, w: (w[1], 0, head(i, w))),
            pl.BlockSpec((1, 2, span, HD), lambda i, w: (jnp.where(i == 0, w[1], docs), 0, 0, 0)),
        ],
        pl.BlockSpec((1, span, width), lambda i, w: (w[1], 0, head(i, w))),
        answer,
        (2,),
        "held",
        cost(2 * GROUPS * span, keys_all, 2 * step_bytes),
    )(where, queries, prefix_keys, prefix_values, doc_keys, doc_values, their_local)

    sent = jax.ShapeDtypeStruct((span, width), jnp.bfloat16)

    def specs(slot):
        query = pl.BlockSpec((1, span, width), lambda i, w: (w[slot + 1], 0, w[0]))
        their_query = pl.BlockSpec((1, span, width), lambda i, w: (slot - 1, 0, 0))
        local = [
            pl.BlockSpec((1, span, HD), lambda i, w: (w[slot + 1], 0, w[0])),
            pl.BlockSpec((1, span, HD), lambda i, w: (w[slot + 1], 0, w[0])),
            pl.BlockSpec((1, 2, span, HD), lambda i, w: (w[slot + 1], 0, 0, 0)),
        ]
        cached = pl.BlockSpec((2, half, HD), lambda i, w: (0, 0, 0))
        mine = pl.BlockSpec((1, span, width), lambda i, w: (w[slot + 1], 0, w[0]))
        theirs = pl.BlockSpec((span, width), lambda i, w: (0, 0))
        return query, their_query, local, cached, mine, theirs

    anywhere = pl.BlockSpec(memory_space=pl.ANY)
    returned = []
    for slot, caches in ((1, (near_first, near_second)), (2, (far_first, far_second))):
        query, their_query, local_specs, cached, mine, theirs = specs(slot)
        out, answer_sent = call(
            functools.partial(both_kernel, 2),
            [query, their_query, *local_specs, cached, cached, anywhere],
            [mine, theirs],
            [answer, sent],
            (2,),
            f"slot{slot}",
            cost(2 * GROUPS * span, keys_all, 2 * step_bytes),
            {8: 0},
        )(where, queries, their_queries, doc_keys, doc_values, their_local, *caches, out)
        returned.append(partner(answer_sent))

    slot = owners - 1
    caches = (middle_first, forward_first, middle_second, forward_second)
    query, their_query, local_specs, cached, mine, theirs = specs(slot)
    answer_sent = call(
        theirs_kernel,
        [their_query, *local_specs, *[cached] * 4],
        theirs,
        sent,
        (1,),
        "last_theirs",
        cost(GROUPS * span, keys_all, step_bytes),
    )(where, their_queries, doc_keys, doc_values, their_local, *caches)
    returned.append(partner(answer_sent))
    out = call(
        mine_kernel,
        [query, *local_specs, *[cached] * 4, anywhere],
        mine,
        answer,
        (1,),
        "last_mine",
        cost(GROUPS * span, keys_all, step_bytes),
        {9: 0},
    )(where, queries, doc_keys, doc_values, their_local, *caches, out)
    for slot, block in enumerate(returned, 1):
        out = lax.dynamic_update_slice(out, block[None], (doc_at[slot], 0, other * width))
    return out


def shards(queries, doc_keys, doc_values, prefix_keys, prefix_values, template, owner_table):
    templates_all = owner_table.shape[0]
    matches = template == jnp.arange(templates_all, dtype=jnp.int32)[None, :]
    holders = jnp.sum(jnp.where(matches, owner_table[None, :], 0), axis=1)
    owners, stages, heads = lax.axis_size("pre"), lax.axis_size("stg"), KVH // lax.axis_size("tp")
    docs, span, _ = queries.shape
    paired = owners == docs == templates_all == 4 and stages == heads == 2
    program = exchanged if paired and span == HD and prefix_keys.shape[1] % (2 * HD) == 0 else gathered
    return program(queries, doc_keys, doc_values, prefix_keys, prefix_values, holders)


def solution(mesh):
    return jax.shard_map(
        shards,
        mesh=mesh,
        in_specs=(
            P(("grp", "pre"), "stg", "tp"),
            P(("grp", "pre"), "stg", "tp"),
            P(("grp", "pre"), "stg", "tp"),
            P(("grp", "pre"), None, "tp"),
            P(("grp", "pre"), None, "tp"),
            P(("grp", "pre"), None),
            P("grp"),
        ),
        out_specs=P(("grp", "pre"), "stg", "tp"),
        check_vma=False,
    )
```

```python
import functools
import math

import jax
import jax.numpy as jnp
from jax import lax
from jax.experimental import pallas as pl
from jax.experimental.pallas import tpu as pltpu
from jax.sharding import PartitionSpec as P

H = 32
KVH = 4
HD = 128
GROUPS = H // KVH
STACK = 2
LOG2_SCALE = HD**-0.5 * math.log2(math.e)
HIDDEN = -1e30
ROWS_BY_FEATURES = (((1,), (1,)), ((), ()))
ROWS_BY_KEYS = (((1,), (0,)), ((), ()))


def prefix_part(rows_in, cache_keys, cache_values, kv_local):
    row_count = rows_in.shape[0]
    groups = H // KVH
    length = cache_keys.shape[0]
    query_heads = rows_in.reshape(row_count, kv_local, groups, HD)
    key_heads = cache_keys.reshape(length, kv_local, HD)
    value_heads = cache_values.reshape(length, kv_local, HD)
    scores = jnp.einsum(
        "tkgh,skh->kgts", query_heads, key_heads, preferred_element_type=jnp.float32
    ) * HD ** (-0.5)
    highest = jnp.max(scores, axis=-1, keepdims=True)
    weights = jnp.exp(scores - highest)
    totals = jnp.sum(weights, axis=-1)
    summed = jnp.einsum(
        "kgts,skh->tkgh",
        weights.astype(jnp.bfloat16),
        value_heads,
        preferred_element_type=jnp.float32,
    )
    output = summed / jnp.transpose(totals, (2, 0, 1))[..., None]
    log_total = jnp.transpose(highest[..., 0] + jnp.log(totals), (2, 0, 1))
    return (
        output.reshape(row_count, kv_local * groups * HD).astype(jnp.bfloat16),
        log_total.reshape(row_count, kv_local * groups),
    )


def gathered(queries, doc_keys, doc_values, prefix_keys, prefix_values, holders):
    kv_local = KVH // lax.axis_size("tp")
    groups = H // KVH
    docs_here, span_len, features = queries.shape
    whole_keys, whole_values = (
        lax.all_gather(prefix_keys, "pre", axis=0, tiled=True),
        lax.all_gather(prefix_values, "pre", axis=0, tiled=True),
    )

    def per_document(packed):
        doc_rows, holder = packed
        cache_keys = lax.dynamic_index_in_dim(whole_keys, holder, 0, keepdims=False)
        cache_values = lax.dynamic_index_in_dim(whole_values, holder, 0, keepdims=False)
        return prefix_part(doc_rows, cache_keys, cache_values, kv_local)

    prefix_rounded, prefix_log = lax.map(per_document, (queries, holders))
    prefix_out = prefix_rounded.astype(jnp.float32)
    query_heads = queries.reshape(docs_here, span_len, kv_local, groups, HD)
    query_pos = lax.axis_index("stg") * span_len + jnp.arange(span_len, dtype=jnp.int32)
    running_max = jnp.full((docs_here, kv_local, groups, span_len), -1e30, jnp.float32)
    key_piece = lax.all_gather(doc_keys, "stg", axis=1, tiled=True)
    value_piece = lax.all_gather(doc_values, "stg", axis=1, tiled=True)
    piece_len = key_piece.shape[1]
    key_heads = key_piece.reshape(docs_here, piece_len, kv_local, HD)
    value_heads = value_piece.reshape(docs_here, piece_len, kv_local, HD)
    scores = jnp.einsum(
        "dtkgh,dskh->dkgts", query_heads, key_heads, preferred_element_type=jnp.float32
    ) * HD ** (-0.5)
    key_pos = jnp.arange(piece_len, dtype=jnp.int32)
    visible = query_pos[:, None] >= key_pos[None, :]
    scores = jnp.where(visible, scores, -1e30)
    new_max = jnp.maximum(running_max, jnp.max(scores, axis=-1))
    weights = jnp.where(visible, jnp.exp(scores - new_max[..., None]), 0.0)
    new_sum = jnp.sum(weights, axis=-1)
    added = jnp.einsum(
        "dkgts,dskh->dkgth",
        weights.astype(jnp.bfloat16),
        value_heads,
        preferred_element_type=jnp.float32,
    )
    local_heads = jnp.transpose(added / new_sum[..., None], (0, 3, 1, 2, 4))
    local_log = jnp.transpose(new_max + jnp.log(new_sum), (0, 3, 1, 2))
    prefix_heads = prefix_out.reshape(docs_here, span_len, kv_local, groups, HD)
    prefix_log = prefix_log.reshape(docs_here, span_len, kv_local, groups)
    joint_log = jnp.logaddexp(prefix_log, local_log)
    mixture = (
        jnp.exp(prefix_log - joint_log)[..., None] * prefix_heads
        + jnp.exp(local_log - joint_log)[..., None] * local_heads
    )
    return mixture.reshape(docs_here, span_len, features).astype(jnp.bfloat16)


def head_slice(column):
    return pl.ds(pl.multiple_of(column, HD), HD)


def attend_kernel(plan, length, where, queries, *refs):
    stage, doc = where[0], where[plan["slot"] + 1]
    other = 1 - stage
    their_queries, refs = (refs[0], refs[1:]) if plan["their_queries"] else (None, refs)
    doc_keys, doc_values, their_local, *caches = refs[: 3 + plan["caches"]]
    refs = refs[3 + plan["caches"] + plan["aliased"] :]
    outs, (rows, keys, values, scores, results, sems) = refs[: plan["outs"]], refs[plan["outs"] :]
    span = doc_keys.shape[1]
    block = scores.shape[1]
    stack = block // span
    parts = plan["parts"]
    used = [0]

    def begin(source, target, ready=None, instead=None):
        sem = sems.at[used[0]]
        used[0] += 1
        copy = pltpu.make_async_copy(source, target, sem)
        if ready is None:
            copy.start()
        else:
            pl.when(ready)(copy.start)
            pl.when(jnp.logical_not(ready))(pltpu.make_async_copy(instead, target, sem).start)
        return copy

    def fetch_rows(at, mine, head):
        source = queries.at[doc] if mine else their_queries.at[plan["sent_at"]]
        base = head * (GROUPS * HD) if mine else 0
        return [
            begin(source.at[:, head_slice(base + g * HD)], rows.at[at, g * span : (g + 1) * span]) for g in range(GROUPS)
        ]

    def fetch_side(side, at, head):
        target, local = ((keys, doc_keys), (values, doc_values))[side]
        cut = slice(0, HD)
        copies = []
        if plan["slot"] == 0:
            copies.append(begin(caches[side].at[0, :, head_slice(head * HD)], target.at[at, :length, cut]))
            theirs = doc if at == 0 else plan["extra"]
        elif plan["slot"] == 3:
            half = length // 2
            for i in range(2):
                copies.append(
                    begin(
                        caches[i].at[side],
                        target.at[at, i * half : (i + 1) * half, cut],
                        where[5] > 0,
                        caches[2].at[side, i * half : (i + 1) * half],
                    )
                )
            theirs = doc
        else:
            size = length // len(caches)
            for i, cache in enumerate(caches):
                copies.append(begin(cache.at[side], target.at[at, i * size : (i + 1) * size, cut]))
            theirs = doc
        copies.append(begin(local.at[doc, :, head_slice(head * HD)], target.at[at, length : length + span, cut]))
        copies.append(begin(their_local.at[theirs, side], target.at[at, length + span :, cut]))
        return copies

    row_copies, key_copies, value_copies = {}, {}, {}
    for at, (mine, own_head) in enumerate(parts):
        head = stage if own_head else other
        row_copies[at] = fetch_rows(at, mine, head)
        if at < keys.shape[0]:
            key_copies[at] = fetch_side(0, at, head)
            value_copies[at] = fetch_side(1, at, head)
    values[:, :, HD:] = jnp.ones(values.shape[:2] + (HD,), values.dtype)

    line = lax.broadcasted_iota(jnp.int32, (block, span), 0) % span
    column = lax.broadcasted_iota(jnp.int32, (block, span), 1)
    causal = line >= column

    def score(number):
        at, first = divmod(number, GROUPS // stack)
        mine = parts[at][0]
        held = min(at, keys.shape[0] - 1)
        for copies in (row_copies, key_copies):
            for copy in copies.pop(at, ()):
                copy.wait()
        query = rows[at, first * block : (first + 1) * block]
        made = lax.dot_general(query, keys[held], ROWS_BY_FEATURES, preferred_element_type=jnp.float32)
        earlier = line * 0 + (stage if mine else other) > 0
        own, theirs = (causal, earlier) if mine else (earlier, causal)
        slot = number % 2
        scores[slot, :, :length] = made[:, :length]
        scores[slot, :, length : length + span] = jnp.where(own, made[:, length : length + span], HIDDEN)
        scores[slot, :, length + span :] = jnp.where(theirs, made[:, length + span :], HIDDEN)

    def weigh(number):
        at, first = divmod(number, GROUPS // stack)
        held = min(at, keys.shape[0] - 1)
        for copy in value_copies.pop(at, ()):
            copy.wait()
        made = scores[number % 2]
        peak = made[:, :HD]
        for start in range(HD, made.shape[1], HD):
            peak = jnp.maximum(peak, made[:, start : start + HD])
        peak = jnp.max(peak, axis=-1, keepdims=True) * LOG2_SCALE
        weights = jnp.exp2(made * LOG2_SCALE - peak).astype(jnp.bfloat16)
        added = lax.dot_general(weights, values[held], ROWS_BY_KEYS, preferred_element_type=jnp.float32)
        result = (added[:, :HD] / added[:, HD:]).astype(jnp.bfloat16)
        for i in range(stack):
            group = first * stack + i
            results[at, :, group * HD : (group + 1) * HD] = result[i * span : (i + 1) * span]

    blocks = len(parts) * GROUPS // stack
    finished = []
    score(0)
    for number in range(blocks):
        if number + 1 < blocks:
            score(number + 1)
        weigh(number)
        at, first = divmod(number, GROUPS // stack)
        if first == GROUPS // stack - 1:
            mine, own_head = parts[at]
            if mine:
                head = stage if own_head else other
                width = GROUPS * HD
                target = outs[0].at[doc, :, pl.ds(pl.multiple_of(head * width, width), width)]
            else:
                target = outs[-1]
            finished.append(begin(results.at[at], target))
    for copy in finished:
        copy.wait()


def pack_kernel(template, owner_table, place, queries, doc_keys, doc_values, where, first, rest, local, sems):
    me, stage = place[0], place[1]
    other = 1 - stage
    docs, span, _ = queries.shape
    width = GROUPS * HD
    where[0] = stage
    doc_at = []
    for distance in range(docs):
        found = jnp.int32(0)
        for doc in range(docs):
            found = jnp.where(owner_table[template[doc, 0]] == me ^ distance, doc, found)
        where[distance + 1] = found
        doc_at.append(found)
    where[5] = jnp.where((me == 0) | (me == docs - 1), 1, 0)
    where[6] = me
    where[7] = other
    columns = pl.ds(pl.multiple_of(other * width, width), width)
    theirs, mine = head_slice(other * HD), head_slice(stage * HD)
    copies = [
        (queries.at[doc_at[1], :, columns], first.at[0]),
        (queries.at[doc_at[2], :, columns], rest.at[0]),
        (queries.at[doc_at[3], :, columns], rest.at[1]),
    ]
    for side, source in enumerate((doc_keys, doc_values)):
        for doc in range(docs):
            copies.append((source.at[doc, :, theirs], local.at[doc, side]))
        copies.append((source.at[doc_at[0], :, mine], local.at[docs, side]))
    copies = [pltpu.make_async_copy(a, b, sems.at[i]) for i, (a, b) in enumerate(copies)]
    for copy in copies:
        copy.start()
    for copy in copies:
        copy.wait()


def place_kernel(where, block, _, out):
    out[0] = block[...]


def exchanged(queries, doc_keys, doc_values, prefix_keys, prefix_values, template, owner_table):
    owners = lax.axis_size("pre")
    docs, span, features = queries.shape
    length = prefix_keys.shape[1]
    half = length // 2
    width = GROUPS * HD
    bf16 = jnp.bfloat16

    def over(axis, pairs):
        return lambda block: lax.ppermute(block, axis, pairs)

    near = over("pre", [(i, i ^ 1) for i in range(owners)])
    far = over("pre", [(i, i ^ 2) for i in range(owners)])
    middle = over("pre", [(1, 2), (2, 1)])
    forward = over("pre", [(2, 3), (1, 0)])
    partner = over("stg", [(0, 1), (1, 0)])

    me, stage = lax.axis_index("pre"), lax.axis_index("stg")
    cache = jnp.stack([prefix_keys[0], prefix_values[0]])
    cache = lax.dynamic_slice_in_dim(cache, stage * HD, HD, 2)
    far_first, far_second = far(cache[:, :half]), far(cache[:, half:])
    near_whole = near(cache)

    place = jnp.where(jnp.arange(2, dtype=jnp.int32) == 0, me, stage).astype(jnp.int32)
    anywhere = pl.BlockSpec(memory_space=pl.ANY)
    in_smem = pl.BlockSpec(memory_space=pltpu.SMEM)
    in_vmem = pl.BlockSpec(memory_space=pltpu.VMEM)
    where, first_queries, rest_queries, sent_local = pl.pallas_call(
        pack_kernel,
        in_specs=[in_smem, in_smem, in_smem, anywhere, anywhere, anywhere],
        out_specs=[in_smem, in_vmem, in_vmem, in_vmem],
        out_shape=[
            jax.ShapeDtypeStruct((8,), jnp.int32),
            jax.ShapeDtypeStruct((1, span, width), bf16),
            jax.ShapeDtypeStruct((2, span, width), bf16),
            jax.ShapeDtypeStruct((docs + 1, 2, span, HD), bf16),
        ],
        scratch_shapes=[pltpu.SemaphoreType.DMA((3 + 2 * (docs + 1),))],
        cost_estimate=pl.CostEstimate(flops=0, transcendentals=0, bytes_accessed=8 * span * width * 2),
        name="pack",
    )(template, owner_table, place, queries, doc_keys, doc_values)
    their_local = partner(sent_local)
    their_first = partner(first_queries)
    their_rest = partner(rest_queries)

    cache, far_first = lax.optimization_barrier((cache, far_first))
    middle_whole, forward_first = middle(cache), forward(far_first)
    forward_second = forward(far_second)

    answer = jax.ShapeDtypeStruct(queries.shape, bf16)
    sent = jax.ShapeDtypeStruct((span, width), bf16)
    keys_all = length + 2 * span
    block = STACK * span

    def call(name, slot, parts, their_queries, sent_at, caches, out, outs):
        sets = len(parts) if slot == 0 else 1
        plan = {
            "slot": slot,
            "parts": parts,
            "their_queries": their_queries is not None,
            "sent_at": sent_at,
            "caches": len(caches),
            "aliased": out is not None,
            "outs": len(outs),
            "extra": docs,
        }
        args = [queries] + ([] if their_queries is None else [their_queries])
        args += [doc_keys, doc_values, their_local, *caches] + ([] if out is None else [out])
        copies = len(parts) * (GROUPS + 1) + sets * 2 * (2 + min(2, len(caches)))
        return pl.pallas_call(
            functools.partial(attend_kernel, plan, length),
            grid_spec=pltpu.PrefetchScalarGridSpec(
                num_scalar_prefetch=1,
                grid=(1,),
                in_specs=[anywhere] * len(args),
                out_specs=[anywhere] * len(outs),
                scratch_shapes=[
                    pltpu.VMEM((len(parts), GROUPS * span, HD), bf16),
                    pltpu.VMEM((sets, keys_all, HD), bf16),
                    pltpu.VMEM((sets, keys_all, 2 * HD), bf16),
                    pltpu.VMEM((2, block, keys_all), jnp.float32),
                    pltpu.VMEM((len(parts), span, width), bf16),
                    pltpu.SemaphoreType.DMA((copies,)),
                ],
            ),
            out_shape=outs,
            input_output_aliases={} if out is None else {len(args): 0},
            compiler_params=pltpu.CompilerParams(vmem_limit_bytes=16 << 20),
            cost_estimate=pl.CostEstimate(
                flops=4 * len(parts) * GROUPS * span * keys_all * HD,
                transcendentals=len(parts) * GROUPS * span * keys_all,
                bytes_accessed=len(parts) * 4 * (span * width + keys_all * HD),
            ),
            name=name,
        )(where, *args)

    theirs, mine, mine_other = (False, True), (True, True), (True, False)
    (out,) = call("held", 0, [mine, mine_other], None, 0, (prefix_keys, prefix_values), None, [answer])
    out, first_sent = call("near", 1, [theirs, mine], their_first, 0, (near_whole,), out, [answer, sent])
    first_back = partner(first_sent)
    out, second_sent = call("far", 2, [theirs, mine], their_rest, 0, (far_first, far_second), out, [answer, sent])
    second_back = partner(second_sent)
    last = (forward_first, forward_second, middle_whole)
    (third_sent,) = call("last_theirs", 3, [theirs], their_rest, 1, last, None, [sent])
    third_back = partner(third_sent)
    (out,) = call("last_mine", 3, [mine], None, 0, last, out, [answer])
    for slot, back in ((1, first_back), (2, second_back), (3, third_back)):
        out = pl.pallas_call(
            place_kernel,
            grid_spec=pltpu.PrefetchScalarGridSpec(
                num_scalar_prefetch=1,
                grid=(1,),
                in_specs=[pl.BlockSpec((span, width), lambda i, w: (0, 0)), anywhere],
                out_specs=pl.BlockSpec((1, span, width), lambda i, w, slot=slot: (w[slot + 1], 0, 1 - w[0])),
            ),
            out_shape=answer,
            input_output_aliases={2: 0},
            cost_estimate=pl.CostEstimate(flops=0, transcendentals=0, bytes_accessed=4 * span * width),
            name=f"place{slot}",
        )(where, back, out)
    return out


def shards(queries, doc_keys, doc_values, prefix_keys, prefix_values, template, owner_table):
    templates_all = owner_table.shape[0]
    owners, stages, heads = lax.axis_size("pre"), lax.axis_size("stg"), KVH // lax.axis_size("tp")
    docs, span, _ = queries.shape
    paired = owners == docs == templates_all == 4 and stages == heads == 2
    if paired and span == HD and prefix_keys.shape[1] % (2 * HD) == 0:
        return exchanged(queries, doc_keys, doc_values, prefix_keys, prefix_values, template, owner_table)
    matches = template == jnp.arange(templates_all, dtype=jnp.int32)[None, :]
    holders = jnp.sum(jnp.where(matches, owner_table[None, :], 0), axis=1)
    return gathered(queries, doc_keys, doc_values, prefix_keys, prefix_values, holders)


def solution(mesh):
    return jax.shard_map(
        shards,
        mesh=mesh,
        in_specs=(
            P(("grp", "pre"), "stg", "tp"),
            P(("grp", "pre"), "stg", "tp"),
            P(("grp", "pre"), "stg", "tp"),
            P(("grp", "pre"), None, "tp"),
            P(("grp", "pre"), None, "tp"),
            P(("grp", "pre"), None),
            P("grp"),
        ),
        out_specs=P(("grp", "pre"), "stg", "tp"),
        check_vma=False,
    )
```
